32 devices in a mesh: grp: 16 (over z, y, x), node: 2 (over core).
Axes of the slice: x: 2, y: 2, z: 4, core: 2. Of those that a mesh axis runs over, the one named last changes fastest.
Arguments:
- tokens: bfloat16 [4096, 2048], P(('grp', 'node')), may hold values from -6 to 6
- codes: bfloat16 [768, 2048], P(('grp', 'node')), may hold values from -3 to 3
- scales: float32 [768, 16], P(('grp', 'node')), may hold values from 0.25 to 4, as said below
- cotangent: bfloat16 [4096, 768], P(('grp', 'node')), may hold values from -6 to 6
Outputs:
- values: bfloat16 [4096, 768], P(('grp', 'node'))
- input_grad: bfloat16 [4096, 2048], P(('grp', 'node'))
- weight_grad: float32 [768, 2048], P(('grp', 'node'))
The draws below stay inside these ranges and needn't reach their ends.
Inputs may be any that keep to these rules, and one draw needn't show every extreme that they name: Positive block scales.
All inputs are finite; a program needn't handle non-finite values.
Results may differ from the reference program's by a relative error of at most 0.012.
Values may be sent and summed in bfloat16 or wider, within the bound.
No kernel may reach another device: no remote copies, remote signals or barrier semaphores. Data moves between devices by JAX's collectives and lax.ppermute only.
A program may use at most 64 MiB of HBM per device.

```python
import math
import jax
import jax.numpy as jnp
from jax import lax

H = 768
D = 2048
QB = 128
TOK_DEV = 128
TOKENS = 4096
N_GRP = 16
N_NODE = 2


def draw_codes(key, part):
    first = jax.random.fold_in(key, 11)
    codes = jnp.clip(jax.random.normal(first, (H, D), jnp.float32), -3.0, 3.0)
    return codes.astype(jnp.bfloat16)


def draw_scales(key, part):
    second = jax.random.fold_in(key, 12)
    lower, upper = (math.log(0.5), math.log(2.0))
    return jnp.exp(jax.random.uniform(second, (H, D // QB), jnp.float32, lower, upper))


def strengthened(array, key, source, target, shards_of, factor):
    owner, partner = [(jnp.arange(array.shape[position]) // (array.shape[position] // shards_of)).reshape([-1 if axis == position else 1 for axis in range(array.ndim)]) for position in (source, target)]
    chosen = jax.random.permutation(key, shards_of)[partner]
    strong = (owner == chosen) | (owner == (partner + shards_of // 2) % shards_of)
    return jnp.where(strong, factor * array, array)


def shard_levels(rng, extent, cuts, least, high):
    factor_of = 1.0
    for dim, parts in cuts:
        steps = jax.random.uniform(jax.random.fold_in(jax.random.fold_in(rng, 6), dim), (parts,), jnp.float32, least / len(cuts), high / len(cuts))
        factor_of = factor_of * jnp.repeat(jnp.exp(steps), extent[dim] // parts).reshape((-1,) + (1,) * (len(extent) - 1 - dim))
    return factor_of


def centred(own_key, extent, deviation, limit, pieces=(), dtype=jnp.bfloat16):
    entries = deviation * jax.random.normal(own_key, extent, jnp.float32)
    if pieces:
        entries = entries * shard_levels(own_key, extent, pieces, -0.22, 0.18)
    return jnp.clip(entries, -limit, limit).astype(dtype)


def noise_with(stream_key, extent, spread, most, pieces, heavy, dtype=jnp.bfloat16):
    array = spread * jax.random.normal(stream_key, extent, jnp.float32)
    if pieces:
        array = array * shard_levels(stream_key, extent, pieces, -0.22, 0.18)
    return jnp.clip(strengthened(array, jax.random.fold_in(stream_key, 3), *heavy), -most, most).astype(dtype)


def setup_inputs(seed: int = 0) -> dict:
    splits = jax.random.split(jax.random.key(seed), 5)
    return {
        "tokens": centred(splits[0], (TOKENS, D), 1.0, 6.0, ((0, 32),)),
        "codes": draw_codes(jax.random.fold_in(splits[4], 71), 0),
        "scales": draw_scales(jax.random.fold_in(splits[4], 71), 0),
        "cotangent": noise_with(splits[3], (TOKENS, H), 1.0, 6.0, ((0, 32),), (0, 1, 32, 2.75)),
    }


def reference(tokens, codes, scales, cotangent):
    floats = tokens.astype(jnp.float32)
    power = lax.optimization_barrier(jnp.mean(floats * floats, axis=-1, keepdims=True))
    normed = (floats * lax.rsqrt(power + 1e-05)).astype(jnp.bfloat16)
    inv_root = D ** (-0.5)
    weight = (codes.astype(jnp.float32).reshape(H, D // QB, QB) * scales[:, :, None] * inv_root).reshape(H, D).astype(jnp.bfloat16)
    values = jnp.dot(normed, weight.T, preferred_element_type=jnp.float32).astype(jnp.bfloat16)
    input_grad = jnp.dot(cotangent, weight, preferred_element_type=jnp.float32).astype(jnp.bfloat16)
    factor = (TOK_DEV * N_GRP * N_NODE) ** (-0.5)
    normed_blocks = normed.reshape(N_GRP * N_NODE, TOK_DEV, D)
    cot_blocks = cotangent.reshape(N_GRP * N_NODE, TOK_DEV, H)

    def accumulate(total, pair):
        term = jnp.dot(pair[1].T, pair[0], preferred_element_type=jnp.float32) * factor
        rounded = lax.optimization_barrier(term.astype(jnp.bfloat16))
        return (total + rounded.astype(jnp.float32), None)
    weight_grad, _ = lax.scan(accumulate, jnp.zeros((H, D), jnp.float32), (normed_blocks, cot_blocks))
    return (values, input_grad, weight_grad)
```

```python
import jax
import jax.numpy as jnp
from jax import lax
from jax.experimental import pallas as pl
from jax.experimental.pallas import tpu as pltpu
from jax.sharding import PartitionSpec as P


AXES = ("grp", "node")
F32 = jnp.float32
BF16 = jnp.bfloat16
VMEM = pl.BlockSpec(memory_space=pltpu.VMEM)
GRANT = 12 * 1024 * 1024


def dequantize(block_codes, block_scales):
    count, width = block_codes.shape
    blocks = block_scales.shape[1]
    floats = (
        block_codes.astype(F32).reshape(count, blocks, -1)
        * block_scales[:, :, None]
        * width ** (-0.5)
    )
    return floats.reshape(count, -1).astype(BF16)


def plain_body(tokens, codes, scales, cotangent):
    rows_here = tokens.shape[0]
    groups = lax.axis_size("grp")
    nodes = lax.axis_size("node")
    per_device = codes.shape[0]
    height = cotangent.shape[1]
    floats = tokens.astype(F32)
    power = jnp.mean(floats * floats, axis=-1, keepdims=True)
    normed = (floats * lax.rsqrt(power + 1e-05)).astype(BF16)
    weight = lax.all_gather(dequantize(codes, scales), AXES, axis=0, tiled=True)
    values = jnp.dot(normed, weight.T, preferred_element_type=F32).astype(BF16)
    input_grad = jnp.dot(cotangent, weight, preferred_element_type=F32).astype(BF16)
    reordered = (
        cotangent.reshape(rows_here, groups, nodes, per_device)
        .transpose(0, 2, 1, 3)
        .reshape(rows_here, height)
    )
    factor = (rows_here * groups * nodes) ** (-0.5)
    term = jnp.einsum("tr,td->rd", reordered, normed, preferred_element_type=F32) * factor
    node_sum = lax.psum_scatter(
        term.astype(BF16), "node", scatter_dimension=0, tiled=True
    ).astype(F32)
    weight_grad = lax.psum_scatter(node_sum, "grp", scatter_dimension=0, tiled=True)
    return (values, input_grad, weight_grad)


def swap_first():
    return [(g * 2 + c, (g ^ (1 + c)) * 2 + c) for g in range(16) for c in range(2)]


def swap_second():
    return [(g * 2 + c, (g ^ (2 - c)) * 2 + c) for g in range(16) for c in range(2)]


def swap_z(k):
    return [(g * 2 + c, (g ^ (4 * k)) * 2 + c) for g in range(16) for c in range(2)]


def swap_core():
    return [(g * 2 + c, g * 2 + 1 - c) for g in range(16) for c in range(2)]


def dequantize_kernel(codes, scales, out):
    width = codes.shape[1]
    blocks = scales.shape[0]
    block = width // blocks
    inv_root = width ** (-0.5)
    by_row = scales[...].T
    for j in range(blocks):
        part = slice(j * block, (j + 1) * block)
        out[:, part] = (codes[:, part].astype(F32) * by_row[:, j : j + 1] * inv_root).astype(BF16)


def place_of(g, core, first, second, k):
    return (g ^ (first * (1 + core) + second * (2 - core) + 4 * k)) * 2 + core


PAIRS = ((0, 0), (1, 0), (0, 1), (1, 1))


def term_kernel(per, factor, tok, tok2, cot, cot2, sent, kept_cot, normed, early, late, cot_t):
    rows = tok.shape[0]
    half = 8 * per
    g = lax.axis_index("grp")
    c = lax.axis_index("node")
    cot_t[:, :rows] = cot[...].astype(F32).T
    cot_t[:, rows:] = cot2[...].astype(F32).T

    def block(core, first, second, k):
        start = pl.multiple_of(place_of(g, core, first, second, k) * per, 8)
        return cot_t[pl.ds(start, per), :]

    def picked(core, first, second):
        return jnp.concatenate([block(core, first, second, k) for k in range(4)], axis=0)

    for i, source in enumerate((tok, tok2)):
        floats = source[...].astype(F32)
        power = jnp.mean(floats * floats, axis=-1, keepdims=True)
        normed[i * rows : (i + 1) * rows, :] = (floats * lax.rsqrt(power + 1e-05)).astype(BF16)
    mine = [picked(c, first, second).astype(BF16) for first, second in PAIRS]
    other = [picked(1 - c, first, second)[:, :rows].astype(BF16) for first, second in PAIRS]
    kept_cot[: half // 2, :] = mine[0]
    kept_cot[half // 2 :, :] = mine[2]
    sent[...] = (
        jnp.dot(
            jnp.concatenate([mine[1], mine[3]], axis=0), normed[...], preferred_element_type=F32
        )
        * factor
    ).astype(BF16)
    for i in range(3):
        early[i * 4 * per : (i + 1) * 4 * per, :] = mine[i][:, :rows]
        early[(i + 3) * 4 * per : (i + 4) * 4 * per, :] = other[i]
    late[: 4 * per, :] = mine[3][:, :rows]
    late[4 * per :, :] = other[3]


def kept_kernel(factor, kept_cot, normed, near, far):
    half = near.shape[0]
    both = jnp.dot(kept_cot[...], normed[...], preferred_element_type=F32) * factor
    near[...] = both[:half, :]
    far[...] = both[half:, :]


def second_kernel(far, got, sent):
    half = sent.shape[0]
    sent[...] = (far[...] + got[half:, :].astype(F32)).astype(BF16)


def spread_kernel(near, got, got2, own, s1, s2, s3):
    per = own.shape[0]
    for k, out in enumerate((own, s1, s2, s3)):
        part = slice(k * per, (k + 1) * per)
        total = near[part, :] + got[part, :].astype(F32) + got2[part, :].astype(F32)
        out[...] = total.astype(out.dtype)


def total_kernel(own, g1, g2, g3, out):
    out[...] = own[...] + g1[...].astype(F32) + g2[...].astype(F32) + g3[...].astype(F32)


def join_kernel(w0, w1, w2, w3, out):
    per = w0.shape[0]
    for k, piece in enumerate((w0, w1, w2, w3)):
        out[k * per : (k + 1) * per, :] = piece[...]


LAST = (((1,), (1,)), ((), ()))
FIRST = (((0,), (0,)), ((), ()))


def early_kernel(normed, cot, w0, w1, w2, w3, w4, w5, values_t, grad, joined):
    count = w0.shape[0]
    rows = grad.shape[0]
    for i, piece in enumerate((w0, w1, w2, w3, w4, w5)):
        joined[i * count : (i + 1) * count, :] = piece[...]
    values_t[...] = lax.dot_general(
        joined[...], normed[:rows, :], LAST, preferred_element_type=F32
    )
    grad[...] = lax.dot_general(cot[...], joined[...], FIRST, preferred_element_type=F32)


def late_kernel(per, normed, cot, w0, w1, values_t, grad, values, input_grad, joined, full_t):
    count = w0.shape[0]
    rows = grad.shape[0]
    g = lax.axis_index("grp")
    c = lax.axis_index("node")
    joined[:count, :] = w0[...]
    joined[count:, :] = w1[...]
    late_t = lax.dot_general(joined[...], normed[:rows, :], LAST, preferred_element_type=F32)
    for i in range(4):
        for j in range(2):
            core = c if j == 0 else 1 - c
            for k in range(4):
                start = pl.multiple_of(place_of(g, core, *PAIRS[i], k) * per, 8)
                if i < 3:
                    at = (i + 3 * j) * count + k * per
                    piece = values_t[at : at + per, :]
                else:
                    at = j * count + k * per
                    piece = late_t[at : at + per, :]
                full_t[pl.ds(start, per), :] = piece
    values[...] = full_t[...].T.astype(BF16)
    input_grad[...] = (
        grad[...] + lax.dot_general(cot[...], joined[...], FIRST, preferred_element_type=F32)
    ).astype(BF16)


def plain(rows, columns, dtype):
    return jax.ShapeDtypeStruct((rows, columns), dtype)


def held(rows, columns, dtype):
    return pltpu.VMEM((rows, columns), dtype)


def move(array, pairs):
    return lax.ppermute(array, AXES, pairs)


def call(kernel, outs, *args, scratch=(), hbm=()):
    args = [
        a if i in hbm else pltpu.with_memory_space_constraint(a, pltpu.VMEM)
        for i, a in enumerate(args)
    ]
    return pl.pallas_call(
        kernel,
        out_shape=outs,
        in_specs=[VMEM] * len(args),
        out_specs=jax.tree.map(lambda _: VMEM, outs),
        scratch_shapes=scratch,
        compiler_params=pltpu.CompilerParams(vmem_limit_bytes=GRANT),
    )(*args)


def block_body(tokens, codes, scales, cotangent):
    return block_steps(tokens, codes, scales, cotangent)


def block_steps(tokens, codes, scales, cotangent):
    rows, width = tokens.shape
    height = cotangent.shape[1]
    per = codes.shape[0]
    quarter = 4 * per
    factor = (rows * 32) ** (-0.5)

    tokens2 = move(tokens, swap_core())
    cotangent2 = move(cotangent, swap_core())
    own = call(dequantize_kernel, held(per, width, BF16), codes, scales.T, hbm=(0, 1))

    sent, kept_cot, normed, early, late = call(
        lambda *refs: term_kernel(per, factor, *refs),
        [
            held(2 * quarter, width, BF16),
            held(2 * quarter, 2 * rows, BF16),
            held(2 * rows, width, BF16),
            held(6 * quarter, rows, BF16),
            held(2 * quarter, rows, BF16),
        ],
        tokens,
        tokens2,
        cotangent,
        cotangent2,
        scratch=[pltpu.VMEM((height, 2 * rows), F32)],
        hbm=(0, 2),
    )
    got = move(sent, swap_first())
    by_z = [own] + [move(own, swap_z(k)) for k in (1, 2, 3)]
    near, far = call(
        lambda *refs: kept_kernel(factor, *refs), [held(quarter, width, F32)] * 2, kept_cot, normed
    )
    w00 = call(join_kernel, held(quarter, width, BF16), *by_z)
    sent2 = call(second_kernel, held(quarter, width, BF16), far, got)
    got2 = move(sent2, swap_second())
    w10 = move(w00, swap_first())
    w01 = move(w00, swap_second())
    v00 = move(w00, swap_core())
    w11 = move(w10, swap_second())
    v10 = move(w10, swap_core())
    v01 = move(w01, swap_core())

    mine, s1, s2, s3 = call(
        spread_kernel, [held(per, width, F32)] + [held(per, width, BF16)] * 3, near, got, got2
    )
    back = [move(s, swap_z(k)) for k, s in ((1, s1), (2, s2), (3, s3))]
    values_t, grad = call(
        early_kernel,
        [held(6 * quarter, rows, F32), held(rows, width, F32)],
        normed,
        early,
        w00,
        w10,
        w01,
        v00,
        v10,
        v01,
        scratch=[pltpu.VMEM((6 * quarter, width), BF16)],
    )
    v11 = move(w11, swap_core())
    values, input_grad = call(
        lambda *refs: late_kernel(per, *refs),
        [plain(rows, height, BF16), plain(rows, width, BF16)],
        normed,
        late,
        w11,
        v11,
        values_t,
        grad,
        scratch=[pltpu.VMEM((2 * quarter, width), BF16), pltpu.VMEM((height, rows), F32)],
    )
    weight_grad = call(total_kernel, plain(per, width, F32), mine, *back)
    return (values, input_grad, weight_grad)


def solution(mesh):
    sizes = dict(mesh.shape)
    blocked = (sizes["grp"], sizes["node"]) == (16, 2)
    split = P(AXES, None)
    return jax.shard_map(
        block_body if blocked else plain_body,
        mesh=mesh,
        in_specs=(split,) * 4,
        out_specs=(split,) * 3,
        check_vma=False,
    )
```

```python
import jax
import jax.numpy as jnp
from jax import lax
from jax.experimental import pallas as pl
from jax.experimental.pallas import tpu as pltpu
from jax.sharding import PartitionSpec as P


AXES = ("grp", "node")
F32 = jnp.float32
BF16 = jnp.bfloat16
VMEM = pl.BlockSpec(memory_space=pltpu.VMEM)
FAR = pl.BlockSpec(memory_space=pltpu.HBM)
GRANT = 12 * 1024 * 1024


def dequantize(block_codes, block_scales):
    count, width = block_codes.shape
    blocks = block_scales.shape[1]
    floats = (
        block_codes.astype(F32).reshape(count, blocks, -1)
        * block_scales[:, :, None]
        * width ** (-0.5)
    )
    return floats.reshape(count, -1).astype(BF16)


def plain_body(tokens, codes, scales, cotangent):
    rows_here = tokens.shape[0]
    groups = lax.axis_size("grp")
    nodes = lax.axis_size("node")
    per_device = codes.shape[0]
    height = cotangent.shape[1]
    floats = tokens.astype(F32)
    power = jnp.mean(floats * floats, axis=-1, keepdims=True)
    normed = (floats * lax.rsqrt(power + 1e-05)).astype(BF16)
    weight = lax.all_gather(dequantize(codes, scales), AXES, axis=0, tiled=True)
    values = jnp.dot(normed, weight.T, preferred_element_type=F32).astype(BF16)
    input_grad = jnp.dot(cotangent, weight, preferred_element_type=F32).astype(BF16)
    reordered = (
        cotangent.reshape(rows_here, groups, nodes, per_device)
        .transpose(0, 2, 1, 3)
        .reshape(rows_here, height)
    )
    factor = (rows_here * groups * nodes) ** (-0.5)
    term = jnp.einsum("tr,td->rd", reordered, normed, preferred_element_type=F32) * factor
    node_sum = lax.psum_scatter(
        term.astype(BF16), "node", scatter_dimension=0, tiled=True
    ).astype(F32)
    weight_grad = lax.psum_scatter(node_sum, "grp", scatter_dimension=0, tiled=True)
    return (values, input_grad, weight_grad)


def swap_first():
    return [(g * 2 + c, (g ^ (1 + c)) * 2 + c) for g in range(16) for c in range(2)]


def swap_second():
    return [(g * 2 + c, (g ^ (2 - c)) * 2 + c) for g in range(16) for c in range(2)]


def swap_z(k):
    return [(g * 2 + c, (g ^ (4 * k)) * 2 + c) for g in range(16) for c in range(2)]


def swap_core():
    return [(g * 2 + c, g * 2 + 1 - c) for g in range(16) for c in range(2)]


def place_of(g, core, first, second, k):
    return (g ^ (first * (1 + core) + second * (2 - core) + 4 * k)) * 2 + core


PAIRS = ((0, 0), (1, 0), (0, 1), (1, 1))


def normalized(tok):
    floats = tok[...].astype(F32)
    power = jnp.mean(floats * floats, axis=-1, keepdims=True)
    return (floats * lax.rsqrt(power + 1e-05)).astype(BF16)


def own_kernel(
    per,
    tok_far,
    cot_far,
    codes_far,
    scales_far,
    weight,
    normed,
    early,
    late,
    cot_t,
    tok,
    cot,
    codes,
    scales,
    sem,
):
    pairs = ((codes_far, codes), (scales_far, scales), (cot_far, cot), (tok_far, tok))
    loads = [pltpu.make_async_copy(x, y, sem.at[i]) for i, (x, y) in enumerate(pairs)]
    for load in loads:
        load.start()
    g = lax.axis_index("grp")
    c = lax.axis_index("node")
    width = tok.shape[1]
    blocks = scales.shape[0]
    block = width // blocks
    inv_root = width ** (-0.5)
    loads[0].wait()
    loads[1].wait()
    by_row = scales[...].T
    for j in range(blocks):
        part = slice(j * block, (j + 1) * block)
        weight[:, part] = (codes[:, part].astype(F32) * by_row[:, j : j + 1] * inv_root).astype(
            BF16
        )
    loads[2].wait()
    cot_t[...] = cot[...].astype(F32).T
    loads[3].wait()
    normed[...] = normalized(tok)
    for i in range(4):
        for j in range(2):
            core = c if j == 0 else 1 - c
            for k in range(4):
                start = pl.multiple_of(place_of(g, core, *PAIRS[i], k) * per, 8)
                piece = cot_t[pl.ds(start, per), :]
                if i < 3:
                    at = ((i + 3 * j) * 4 + k) * per
                    early[at : at + per, :] = piece
                else:
                    at = (j * 4 + k) * per
                    late[at : at + per, :] = piece


def term_kernel(
    per, factor, tok2, cot2, normed1, early1, late1, sent, kept_cot, normed, early, late, cot_t
):
    rows = tok2.shape[0]
    quarter = 4 * per
    g = lax.axis_index("grp")
    c = lax.axis_index("node")
    normed[:rows, :] = normed1[...]
    normed[rows:, :] = normalized(tok2)
    cot_t[...] = cot2[...].astype(F32).T
    early[...] = early1[...].astype(BF16)
    late[...] = late1[...].astype(BF16)

    def both(i, own):
        first, second = PAIRS[i]
        swapped = [
            cot_t[pl.ds(pl.multiple_of(place_of(g, c, first, second, k) * per, 8), per), :]
            for k in range(4)
        ]
        return jnp.concatenate([own, jnp.concatenate(swapped, axis=0)], axis=1).astype(BF16)

    kept_cot[:quarter, :] = both(0, early1[:quarter, :])
    kept_cot[quarter:, :] = both(2, early1[2 * quarter : 3 * quarter, :])
    going = jnp.concatenate(
        [both(1, early1[quarter : 2 * quarter, :]), both(3, late1[:quarter, :])], axis=0
    )
    sent[...] = (jnp.dot(going, normed[...], preferred_element_type=F32) * factor).astype(BF16)


def kept_kernel(factor, kept_cot, normed, near, far):
    half = near.shape[0]
    both = jnp.dot(kept_cot[...], normed[...], preferred_element_type=F32) * factor
    near[...] = both[:half, :]
    far[...] = both[half:, :]


def second_kernel(far, got, sent):
    half = sent.shape[0]
    sent[...] = (far[...] + got[half:, :].astype(F32)).astype(BF16)


def spread_kernel(near, got, got2, own, s1, s2, s3):
    per = own.shape[0]
    for k, out in enumerate((own, s1, s2, s3)):
        part = slice(k * per, (k + 1) * per)
        total = near[part, :] + got[part, :].astype(F32) + got2[part, :].astype(F32)
        out[...] = total.astype(out.dtype)


def total_kernel(own, g1, g2, g3, out):
    out[...] = own[...] + g1[...].astype(F32) + g2[...].astype(F32) + g3[...].astype(F32)


def join_kernel(w0, w1, w2, w3, out):
    per = w0.shape[0]
    for k, piece in enumerate((w0, w1, w2, w3)):
        out[k * per : (k + 1) * per, :] = piece[...]


LAST = (((1,), (1,)), ((), ()))
FIRST = (((0,), (0,)), ((), ()))


def early_kernel(normed, cot, w0, w1, w2, w3, w4, w5, values_t, grad, joined):
    count = w0.shape[0]
    rows = grad.shape[0]
    for i, piece in enumerate((w0, w1, w2, w3, w4, w5)):
        joined[i * count : (i + 1) * count, :] = piece[...]
    values_t[...] = lax.dot_general(
        joined[...], normed[:rows, :], LAST, preferred_element_type=F32
    )
    grad[...] = lax.dot_general(cot[...], joined[...], FIRST, preferred_element_type=F32)


def late_kernel(per, normed, cot, w0, w1, values_t, grad, values, input_grad, joined, full_t):
    count = w0.shape[0]
    rows = grad.shape[0]
    g = lax.axis_index("grp")
    c = lax.axis_index("node")
    joined[:count, :] = w0[...]
    joined[count:, :] = w1[...]
    late_t = lax.dot_general(joined[...], normed[:rows, :], LAST, preferred_element_type=F32)
    for i in range(4):
        for j in range(2):
            core = c if j == 0 else 1 - c
            for k in range(4):
                start = pl.multiple_of(place_of(g, core, *PAIRS[i], k) * per, 8)
                if i < 3:
                    at = (i + 3 * j) * count + k * per
                    piece = values_t[at : at + per, :]
                else:
                    at = j * count + k * per
                    piece = late_t[at : at + per, :]
                full_t[pl.ds(start, per), :] = piece
    values[...] = full_t[...].T.astype(BF16)
    input_grad[...] = (
        grad[...] + lax.dot_general(cot[...], joined[...], FIRST, preferred_element_type=F32)
    ).astype(BF16)


def plain(rows, columns, dtype):
    return jax.ShapeDtypeStruct((rows, columns), dtype)


def held(rows, columns, dtype):
    return pltpu.VMEM((rows, columns), dtype)


def move(array, pairs):
    return lax.ppermute(array, AXES, pairs)


def call(kernel, outs, *args, scratch=(), far=()):
    args = [
        pltpu.with_memory_space_constraint(a, pltpu.HBM if i in far else pltpu.VMEM)
        for i, a in enumerate(args)
    ]
    return pl.pallas_call(
        kernel,
        out_shape=outs,
        in_specs=[FAR if i in far else VMEM for i in range(len(args))],
        out_specs=jax.tree.map(lambda _: VMEM, outs),
        scratch_shapes=scratch,
        compiler_params=pltpu.CompilerParams(vmem_limit_bytes=GRANT),
    )(*args)


def block_body(tokens, codes, scales, cotangent):
    return block_steps(tokens, codes, scales, cotangent)


def block_steps(tokens, codes, scales, cotangent):
    rows, width = tokens.shape
    height = cotangent.shape[1]
    per = codes.shape[0]
    quarter = 4 * per
    factor = (rows * 32) ** (-0.5)

    tokens2 = move(tokens, swap_core())
    cotangent2 = move(cotangent, swap_core())
    own, normed1, early1, late1 = call(
        lambda *refs: own_kernel(per, *refs),
        [
            held(per, width, BF16),
            held(rows, width, BF16),
            held(6 * quarter, rows, F32),
            held(2 * quarter, rows, F32),
        ],
        tokens,
        cotangent,
        codes,
        scales.T,
        scratch=[
            pltpu.VMEM((height, rows), F32),
            pltpu.VMEM((rows, width), BF16),
            pltpu.VMEM((rows, height), BF16),
            pltpu.VMEM((per, width), BF16),
            pltpu.VMEM((scales.shape[1], per), F32),
            pltpu.SemaphoreType.DMA((4,)),
        ],
        far=(0, 1, 2, 3),
    )
    sent, kept_cot, normed, early, late = call(
        lambda *refs: term_kernel(per, factor, *refs),
        [
            held(2 * quarter, width, BF16),
            held(2 * quarter, 2 * rows, BF16),
            held(2 * rows, width, BF16),
            held(6 * quarter, rows, BF16),
            held(2 * quarter, rows, BF16),
        ],
        tokens2,
        cotangent2,
        normed1,
        early1,
        late1,
        scratch=[pltpu.VMEM((height, rows), F32)],
    )
    got = move(sent, swap_first())
    by_z = [own] + [move(own, swap_z(k)) for k in (1, 2, 3)]
    near, far = call(
        lambda *refs: kept_kernel(factor, *refs), [held(quarter, width, F32)] * 2, kept_cot, normed
    )
    w00 = call(join_kernel, held(quarter, width, BF16), *by_z)
    sent2 = call(second_kernel, held(quarter, width, BF16), far, got)
    got2 = move(sent2, swap_second())
    w10 = move(w00, swap_first())
    w01 = move(w00, swap_second())
    v00 = move(w00, swap_core())
    w11 = move(w01, swap_first())
    v10 = move(w10, swap_core())
    v01 = move(w01, swap_core())

    mine, s1, s2, s3 = call(
        spread_kernel, [held(per, width, F32)] + [held(per, width, BF16)] * 3, near, got, got2
    )
    back = [move(s, swap_z(k)) for k, s in ((1, s1), (2, s2), (3, s3))]
    values_t, grad = call(
        early_kernel,
        [held(6 * quarter, rows, F32), held(rows, width, F32)],
        normed,
        early,
        w00,
        w10,
        w01,
        v00,
        v10,
        v01,
        scratch=[pltpu.VMEM((6 * quarter, width), BF16)],
    )
    v11 = move(w11, swap_core())
    values, input_grad = call(
        lambda *refs: late_kernel(per, *refs),
        [plain(rows, height, BF16), plain(rows, width, BF16)],
        normed,
        late,
        w11,
        v11,
        values_t,
        grad,
        scratch=[pltpu.VMEM((2 * quarter, width), BF16), pltpu.VMEM((height, rows), F32)],
    )
    weight_grad = call(total_kernel, plain(per, width, F32), mine, *back)
    return (values, input_grad, weight_grad)


def solution(mesh):
    sizes = dict(mesh.shape)
    blocked = (sizes["grp"], sizes["node"]) == (16, 2)
    split = P(AXES, None)
    return jax.shard_map(
        block_body if blocked else plain_body,
        mesh=mesh,
        in_specs=(split,) * 4,
        out_specs=(split,) * 3,
        check_vma=False,
    )
```

```python
import jax
import jax.numpy as jnp
from jax import lax
from jax.experimental import pallas as pl
from jax.experimental.pallas import tpu as pltpu
from jax.sharding import PartitionSpec as P


AXES = ("grp", "node")
F32 = jnp.float32
BF16 = jnp.bfloat16
VMEM = pl.BlockSpec(memory_space=pltpu.VMEM)
FAR = pl.BlockSpec(memory_space=pltpu.HBM)
GRANT = 12 * 1024 * 1024


def dequantize(block_codes, block_scales):
    count, width = block_codes.shape
    blocks = block_scales.shape[1]
    floats = (
        block_codes.astype(F32).reshape(count, blocks, -1)
        * block_scales[:, :, None]
        * width ** (-0.5)
    )
    return floats.reshape(count, -1).astype(BF16)


def plain_body(tokens, codes, scales, cotangent):
    rows_here = tokens.shape[0]
    groups = lax.axis_size("grp")
    nodes = lax.axis_size("node")
    per_device = codes.shape[0]
    height = cotangent.shape[1]
    floats = tokens.astype(F32)
    power = jnp.mean(floats * floats, axis=-1, keepdims=True)
    normed = (floats * lax.rsqrt(power + 1e-05)).astype(BF16)
    weight = lax.all_gather(dequantize(codes, scales), AXES, axis=0, tiled=True)
    values = jnp.dot(normed, weight.T, preferred_element_type=F32).astype(BF16)
    input_grad = jnp.dot(cotangent, weight, preferred_element_type=F32).astype(BF16)
    reordered = (
        cotangent.reshape(rows_here, groups, nodes, per_device)
        .transpose(0, 2, 1, 3)
        .reshape(rows_here, height)
    )
    factor = (rows_here * groups * nodes) ** (-0.5)
    term = jnp.einsum("tr,td->rd", reordered, normed, preferred_element_type=F32) * factor
    node_sum = lax.psum_scatter(
        term.astype(BF16), "node", scatter_dimension=0, tiled=True
    ).astype(F32)
    weight_grad = lax.psum_scatter(node_sum, "grp", scatter_dimension=0, tiled=True)
    return (values, input_grad, weight_grad)


def swap_first():
    return [(g * 2 + c, (g ^ (1 + c)) * 2 + c) for g in range(16) for c in range(2)]


def swap_second():
    return [(g * 2 + c, (g ^ (2 - c)) * 2 + c) for g in range(16) for c in range(2)]


def swap_z(k):
    return [(g * 2 + c, (g ^ (4 * k)) * 2 + c) for g in range(16) for c in range(2)]


def swap_core():
    return [(g * 2 + c, g * 2 + 1 - c) for g in range(16) for c in range(2)]


def row_block(g, c, j, block, per):
    core = c if j == 0 else 1 - c
    start = place_of(g, core, *PAIRS[block[0]], block[1]) * per
    return pl.ds(pl.multiple_of(start, 8), per)


def place_of(g, core, first, second, k):
    return (g ^ (first * (1 + core) + second * (2 - core) + 4 * k)) * 2 + core


PAIRS = ((0, 0), (1, 0), (0, 1), (1, 1))
EARLY = tuple((i, k) for i in (0, 2, 1) for k in range(4))
MID = ((3, 0), (3, 1))
LATE = ((3, 2), (3, 3))


def normalized(tok):
    floats = tok[...].astype(F32)
    power = jnp.mean(floats * floats, axis=-1, keepdims=True)
    return (floats * lax.rsqrt(power + 1e-05)).astype(BF16)


def own_kernel(
    per,
    tok_far,
    cot_far,
    codes_far,
    scales_far,
    weight,
    normed,
    early,
    mid,
    late,
    cot_t,
    tok,
    cot,
    codes,
    scales,
    sem,
):
    pairs = ((codes_far, codes), (scales_far, scales), (cot_far, cot), (tok_far, tok))
    loads = [pltpu.make_async_copy(x, y, sem.at[i]) for i, (x, y) in enumerate(pairs)]
    for load in loads:
        load.start()
    g = lax.axis_index("grp")
    c = lax.axis_index("node")
    width = tok.shape[1]
    blocks = scales.shape[0]
    wide = width // blocks
    inv_root = width ** (-0.5)
    loads[0].wait()
    loads[1].wait()
    by_row = scales[...].T
    for j in range(blocks):
        part = slice(j * wide, (j + 1) * wide)
        weight[:, part] = (codes[:, part].astype(F32) * by_row[:, j : j + 1] * inv_root).astype(
            BF16
        )
    loads[2].wait()
    cot_t[...] = cot[...].astype(F32).T
    loads[3].wait()
    normed[...] = normalized(tok)
    for out, blocks in ((early, EARLY), (mid, MID), (late, LATE)):
        for j in range(2):
            for n, block in enumerate(blocks):
                at = (j * len(blocks) + n) * per
                out[at : at + per, :] = cot_t[row_block(g, c, j, block, per), :]


def term_kernel(
    per, factor, tok2, cot2, normed1, early, mid, late, sent, going, kept_cot, normed, cot_t
):
    rows = tok2.shape[0]
    quarter = 4 * per
    g = lax.axis_index("grp")
    c = lax.axis_index("node")
    normed[:rows, :] = normed1[...]
    normed[rows:, :] = normalized(tok2)
    cot_t[...] = cot2[...].astype(F32).T

    def both(i, own):
        swapped = [cot_t[row_block(g, c, 0, (i, k), per), :] for k in range(4)]
        return jnp.concatenate([own, jnp.concatenate(swapped, axis=0)], axis=1).astype(BF16)

    kept_cot[:quarter, :] = both(0, early[:quarter, :])
    kept_cot[quarter:, :] = both(2, early[quarter : 2 * quarter, :])
    going[...] = both(1, early[2 * quarter : 3 * quarter, :])
    last = jnp.concatenate([mid[: 2 * per, :], late[: 2 * per, :]], axis=0)
    sent[...] = (
        jnp.dot(both(3, last), normed[...], preferred_element_type=F32) * factor
    ).astype(BF16)


def kept_kernel(factor, going, kept_cot, normed, *refs):
    (early1, mid1, late1), (sent, near, far, early, mid, late) = refs[:3], refs[3:]
    half = near.shape[0]
    sent[...] = (
        jnp.dot(going[...], normed[...], preferred_element_type=F32) * factor
    ).astype(BF16)
    both = jnp.dot(kept_cot[...], normed[...], preferred_element_type=F32) * factor
    near[...] = both[:half, :]
    far[...] = both[half:, :]
    early[...] = early1[...].astype(BF16)
    mid[...] = mid1[...].astype(BF16)
    late[...] = late1[...].astype(BF16)


def second_kernel(far, got_a, sent):
    sent[...] = (far[...] + got_a[...].astype(F32)).astype(BF16)


def spread_kernel(near, got_b, got2, own, s1, s2, s3):
    per = own.shape[0]
    for k, out in enumerate((own, s1, s2, s3)):
        part = slice(k * per, (k + 1) * per)
        total = near[part, :] + got_b[part, :].astype(F32) + got2[part, :].astype(F32)
        out[...] = total.astype(out.dtype)


def total_kernel(own, g1, g2, g3, out):
    out[...] = own[...] + g1[...].astype(F32) + g2[...].astype(F32) + g3[...].astype(F32)


def join_kernel(w0, w1, w2, w3, out, front, back):
    per = w0.shape[0]
    for k, piece in enumerate((w0, w1, w2, w3)):
        part = slice(k * per, (k + 1) * per)
        half = slice(k % 2 * per, (k % 2 + 1) * per)
        out[part, :] = piece[...]
        (front if k < 2 else back)[half, :] = piece[...]


LAST = (((1,), (1,)), ((), ()))
FIRST = (((0,), (0,)), ((), ()))


def stack(pieces, joined):
    at = 0
    for piece in pieces:
        joined[at : at + piece.shape[0], :] = piece[...]
        at += piece.shape[0]


def early_kernel(per, normed, cot, *refs):
    pieces, (full_t, grad, joined) = refs[:8], refs[8:]
    rows = grad.shape[0]
    g = lax.axis_index("grp")
    c = lax.axis_index("node")
    stack(pieces, joined)
    values_t = lax.dot_general(joined[...], normed[:rows, :], LAST, preferred_element_type=F32)
    for j in range(2):
        for n, block in enumerate(EARLY):
            at = (j * len(EARLY) + n) * per
            full_t[row_block(g, c, j, block, per), :] = values_t[at : at + per, :]
        for block in MID + LATE:
            full_t[row_block(g, c, j, block, per), :] = jnp.zeros((per, rows), F32)
    grad[...] = lax.dot_general(cot[...], joined[...], FIRST, preferred_element_type=F32)


def mid_kernel(per, normed, cot, w0, w1, full_t1, grad1, full_t, grad, joined):
    rows = grad.shape[0]
    g = lax.axis_index("grp")
    c = lax.axis_index("node")
    stack((w0, w1), joined)
    values_t = lax.dot_general(joined[...], normed[:rows, :], LAST, preferred_element_type=F32)
    full_t[...] = full_t1[...]
    for j in range(2):
        for n, block in enumerate(MID):
            at = (j * len(MID) + n) * per
            full_t[row_block(g, c, j, block, per), :] = values_t[at : at + per, :]
    grad[...] = grad1[...] + lax.dot_general(
        cot[...], joined[...], FIRST, preferred_element_type=F32
    )


def late_kernel(per, normed, cot, w0, w1, full_t1, grad, values_far, grad_far, *refs):
    joined, full_t, values, out, sem = refs
    rows = grad.shape[0]
    half = out.shape[1] // 2
    g = lax.axis_index("grp")
    c = lax.axis_index("node")
    stores = [
        pltpu.make_async_copy(
            out.at[:, pl.ds(i * half, half)], grad_far.at[:, pl.ds(i * half, half)], sem.at[i]
        )
        for i in range(2)
    ] + [pltpu.make_async_copy(values, values_far, sem.at[2])]
    stack((w0, w1), joined)
    for i in range(2):
        part = slice(i * half, (i + 1) * half)
        out[:, part] = (
            grad[:, part]
            + lax.dot_general(cot[...], joined[:, part], FIRST, preferred_element_type=F32)
        ).astype(BF16)
        stores[i].start()
    values_t = lax.dot_general(joined[...], normed[:rows, :], LAST, preferred_element_type=F32)
    full_t[...] = full_t1[...]
    for j in range(2):
        for n, block in enumerate(LATE):
            at = (j * len(LATE) + n) * per
            full_t[row_block(g, c, j, block, per), :] = values_t[at : at + per, :]
    values[...] = full_t[...].T.astype(BF16)
    stores[2].start()
    for store in stores:
        store.wait()


def plain(rows, columns, dtype):
    return jax.ShapeDtypeStruct((rows, columns), dtype)


def held(rows, columns, dtype):
    return pltpu.VMEM((rows, columns), dtype)


def move(array, pairs):
    return lax.ppermute(array, AXES, pairs)


def call(kernel, outs, *args, scratch=(), far=(), far_outs=False):
    args = [
        pltpu.with_memory_space_constraint(a, pltpu.HBM if i in far else pltpu.VMEM)
        for i, a in enumerate(args)
    ]
    return pl.pallas_call(
        kernel,
        out_shape=outs,
        in_specs=[FAR if i in far else VMEM for i in range(len(args))],
        out_specs=jax.tree.map(lambda _: FAR if far_outs else VMEM, outs),
        scratch_shapes=scratch,
        compiler_params=pltpu.CompilerParams(vmem_limit_bytes=GRANT),
    )(*args)


def block_body(tokens, codes, scales, cotangent):
    return block_steps(tokens, codes, scales, cotangent)


def block_steps(tokens, codes, scales, cotangent):
    rows, width = tokens.shape
    height = cotangent.shape[1]
    per = codes.shape[0]
    quarter = 4 * per
    factor = (rows * 32) ** (-0.5)

    tokens2 = move(tokens, swap_core())
    cotangent2 = move(cotangent, swap_core())
    own, normed1, *cots = call(
        lambda *refs: own_kernel(per, *refs),
        [
            held(per, width, BF16),
            held(rows, width, BF16),
            held(24 * per, rows, F32),
            held(4 * per, rows, F32),
            held(4 * per, rows, F32),
        ],
        tokens,
        cotangent,
        codes,
        scales.T,
        scratch=[
            pltpu.VMEM((height, rows), F32),
            pltpu.VMEM((rows, width), BF16),
            pltpu.VMEM((rows, height), BF16),
            pltpu.VMEM((per, width), BF16),
            pltpu.VMEM((scales.shape[1], per), F32),
            pltpu.SemaphoreType.DMA((4,)),
        ],
        far=(0, 1, 2, 3),
    )
    sent_a, going, kept_cot, normed = call(
        lambda *refs: term_kernel(per, factor, *refs),
        [
            held(quarter, width, BF16),
            held(quarter, 2 * rows, BF16),
            held(2 * quarter, 2 * rows, BF16),
            held(2 * rows, width, BF16),
        ],
        tokens2,
        cotangent2,
        normed1,
        *cots,
        scratch=[pltpu.VMEM((height, rows), F32)],
    )
    got_a = move(sent_a, swap_first())
    by_z = [own] + [move(own, swap_z(k)) for k in (1, 2, 3)]
    sent_b, near, far, early, mid, late = call(
        lambda *refs: kept_kernel(factor, *refs),
        [
            held(quarter, width, BF16),
            held(quarter, width, F32),
            held(quarter, width, F32),
            held(24 * per, rows, BF16),
            held(4 * per, rows, BF16),
            held(4 * per, rows, BF16),
        ],
        going,
        kept_cot,
        normed,
        *cots,
    )
    got_b = move(sent_b, swap_first())
    w00, front, back = call(
        join_kernel, [held(quarter, width, BF16)] + [held(2 * per, width, BF16)] * 2, *by_z
    )
    sent2 = call(second_kernel, held(quarter, width, BF16), far, got_a)
    got2 = move(sent2, swap_second())
    w01a = move(front, swap_second())
    w01b = move(back, swap_second())
    w10 = move(w00, swap_first())
    w11a = move(w01a, swap_first())
    w11b = move(w01b, swap_first())
    v00 = move(w00, swap_core())
    v01a = move(w01a, swap_core())
    v01b = move(w01b, swap_core())
    v10 = move(w10, swap_core())

    mine, s1, s2, s3 = call(
        spread_kernel, [held(per, width, F32)] + [held(per, width, BF16)] * 3, near, got_b, got2
    )
    others = [move(s, swap_z(k)) for k, s in ((1, s1), (2, s2), (3, s3))]
    full_t, grad = call(
        lambda *refs: early_kernel(per, *refs),
        [held(height, rows, F32), held(rows, width, F32)],
        normed,
        early,
        w00,
        w01a,
        w01b,
        w10,
        v00,
        v01a,
        v01b,
        v10,
        scratch=[pltpu.VMEM((24 * per, width), BF16)],
    )
    v11a = move(w11a, swap_core())
    full_t, grad = call(
        lambda *refs: mid_kernel(per, *refs),
        [held(height, rows, F32), held(rows, width, F32)],
        normed,
        mid,
        w11a,
        v11a,
        full_t,
        grad,
        scratch=[pltpu.VMEM((4 * per, width), BF16)],
    )
    v11b = move(w11b, swap_core())
    values, input_grad = call(
        lambda *refs: late_kernel(per, *refs),
        [plain(rows, height, BF16), plain(rows, width, BF16)],
        normed,
        late,
        w11b,
        v11b,
        full_t,
        grad,
        scratch=[
            pltpu.VMEM((4 * per, width), BF16),
            pltpu.VMEM((height, rows), F32),
            pltpu.VMEM((rows, height), BF16),
            pltpu.VMEM((rows, width), BF16),
            pltpu.SemaphoreType.DMA((3,)),
        ],
        far_outs=True,
    )
    weight_grad = call(total_kernel, plain(per, width, F32), mine, *others)
    return (values, input_grad, weight_grad)


def solution(mesh):
    sizes = dict(mesh.shape)
    blocked = (sizes["grp"], sizes["node"]) == (16, 2)
    split = P(AXES, None)
    return jax.shard_map(
        block_body if blocked else plain_body,
        mesh=mesh,
        in_specs=(split,) * 4,
        out_specs=(split,) * 3,
        check_vma=False,
    )
```

```python
import jax
import jax.numpy as jnp
from jax import lax
from jax.experimental import pallas as pl
from jax.experimental.pallas import tpu as pltpu
from jax.sharding import PartitionSpec as P


AXES = ("grp", "node")
F32 = jnp.float32
BF16 = jnp.bfloat16
VMEM = pl.BlockSpec(memory_space=pltpu.VMEM)
FAR = pl.BlockSpec(memory_space=pltpu.HBM)
GRANT = 12 * 1024 * 1024


def dequantize(block_codes, block_scales):
    count, width = block_codes.shape
    blocks = block_scales.shape[1]
    floats = (
        block_codes.astype(F32).reshape(count, blocks, -1)
        * block_scales[:, :, None]
        * width ** (-0.5)
    )
    return floats.reshape(count, -1).astype(BF16)


def plain_body(tokens, codes, scales, cotangent):
    rows_here = tokens.shape[0]
    groups = lax.axis_size("grp")
    nodes = lax.axis_size("node")
    per_device = codes.shape[0]
    height = cotangent.shape[1]
    floats = tokens.astype(F32)
    power = jnp.mean(floats * floats, axis=-1, keepdims=True)
    normed = (floats * lax.rsqrt(power + 1e-05)).astype(BF16)
    weight = lax.all_gather(dequantize(codes, scales), AXES, axis=0, tiled=True)
    values = jnp.dot(normed, weight.T, preferred_element_type=F32).astype(BF16)
    input_grad = jnp.dot(cotangent, weight, preferred_element_type=F32).astype(BF16)
    reordered = (
        cotangent.reshape(rows_here, groups, nodes, per_device)
        .transpose(0, 2, 1, 3)
        .reshape(rows_here, height)
    )
    factor = (rows_here * groups * nodes) ** (-0.5)
    term = jnp.einsum("tr,td->rd", reordered, normed, preferred_element_type=F32) * factor
    node_sum = lax.psum_scatter(
        term.astype(BF16), "node", scatter_dimension=0, tiled=True
    ).astype(F32)
    weight_grad = lax.psum_scatter(node_sum, "grp", scatter_dimension=0, tiled=True)
    return (values, input_grad, weight_grad)


def swap_first():
    return [(g * 2 + c, (g ^ (1 + c)) * 2 + c) for g in range(16) for c in range(2)]


def swap_second():
    return [(g * 2 + c, (g ^ (2 - c)) * 2 + c) for g in range(16) for c in range(2)]


def swap_z(k):
    return [(g * 2 + c, (g ^ (4 * k)) * 2 + c) for g in range(16) for c in range(2)]


def swap_core():
    return [(g * 2 + c, g * 2 + 1 - c) for g in range(16) for c in range(2)]


def row_block(g, c, j, block, per):
    core = c if j == 0 else 1 - c
    start = place_of(g, core, *PAIRS[block[0]], block[1]) * per
    return pl.ds(pl.multiple_of(start, 8), per)


def place_of(g, core, first, second, k):
    return (g ^ (first * (1 + core) + second * (2 - core) + 4 * k)) * 2 + core


PAIRS = ((0, 0), (1, 0), (0, 1), (1, 1))
EARLY = tuple((i, k) for i in (0, 2, 1) for k in range(4))
MID = ((3, 0), (3, 1))
LATE = ((3, 2), (3, 3))


def normalized(tok):
    floats = tok[...].astype(F32)
    power = jnp.mean(floats * floats, axis=-1, keepdims=True)
    return (floats * lax.rsqrt(power + 1e-05)).astype(BF16)


def own_kernel(
    per,
    tok_far,
    cot_far,
    codes_far,
    scales_far,
    weight,
    normed,
    early,
    mid,
    late,
    cot_t,
    tok,
    cot,
    codes,
    scales,
    sem,
):
    pairs = ((codes_far, codes), (scales_far, scales), (cot_far, cot), (tok_far, tok))
    loads = [pltpu.make_async_copy(x, y, sem.at[i]) for i, (x, y) in enumerate(pairs)]
    for load in loads:
        load.start()
    g = lax.axis_index("grp")
    c = lax.axis_index("node")
    width = tok.shape[1]
    blocks = scales.shape[0]
    wide = width // blocks
    inv_root = width ** (-0.5)
    loads[0].wait()
    loads[1].wait()
    by_row = scales[...].T
    for j in range(blocks):
        part = slice(j * wide, (j + 1) * wide)
        weight[:, part] = (codes[:, part].astype(F32) * by_row[:, j : j + 1] * inv_root).astype(
            BF16
        )
    loads[2].wait()
    cot_t[...] = cot[...].astype(F32).T
    loads[3].wait()
    normed[...] = normalized(tok)
    for out, blocks in ((early, EARLY), (mid, MID), (late, LATE)):
        for j in range(2):
            for n, block in enumerate(blocks):
                at = (j * len(blocks) + n) * per
                out[at : at + per, :] = cot_t[row_block(g, c, j, block, per), :]


def term_kernel(
    per, factor, tok2, cot2, normed1, early, mid, late, sent, going, kept_cot, normed, cot_t
):
    rows = tok2.shape[0]
    quarter = 4 * per
    g = lax.axis_index("grp")
    c = lax.axis_index("node")
    normed[:rows, :] = normed1[...]
    normed[rows:, :] = normalized(tok2)
    cot_t[...] = cot2[...].astype(F32).T

    def both(i, own):
        swapped = [cot_t[row_block(g, c, 0, (i, k), per), :] for k in range(4)]
        return jnp.concatenate([own, jnp.concatenate(swapped, axis=0)], axis=1).astype(BF16)

    kept_cot[:quarter, :] = both(0, early[:quarter, :])
    kept_cot[quarter:, :] = both(2, early[quarter : 2 * quarter, :])
    going[...] = both(1, early[2 * quarter : 3 * quarter, :])
    last = jnp.concatenate([mid[: 2 * per, :], late[: 2 * per, :]], axis=0)
    sent[...] = (
        jnp.dot(both(3, last), normed[...], preferred_element_type=F32) * factor
    ).astype(BF16)


def kept_kernel(factor, going, kept_cot, normed, *refs):
    (early1, mid1, late1), (sent, near, far, early, mid, late) = refs[:3], refs[3:]
    half = near.shape[0]
    sent[...] = (
        jnp.dot(going[...], normed[...], preferred_element_type=F32) * factor
    ).astype(BF16)
    both = jnp.dot(kept_cot[...], normed[...], preferred_element_type=F32) * factor
    near[...] = both[:half, :]
    far[...] = both[half:, :]
    early[...] = early1[...].astype(BF16)
    mid[...] = mid1[...].astype(BF16)
    late[...] = late1[...].astype(BF16)


def second_kernel(far, got_a, sent):
    sent[...] = (far[...] + got_a[...].astype(F32)).astype(BF16)


def spread_kernel(near, got_b, got2, own, s1, s2, s3):
    per = own.shape[0]
    for k, out in enumerate((own, s1, s2, s3)):
        part = slice(k * per, (k + 1) * per)
        total = near[part, :] + got_b[part, :].astype(F32) + got2[part, :].astype(F32)
        out[...] = total.astype(out.dtype)


def join_kernel(w0, w1, w2, w3, out, front, back):
    per = w0.shape[0]
    for k, piece in enumerate((w0, w1, w2, w3)):
        part = slice(k * per, (k + 1) * per)
        half = slice(k % 2 * per, (k % 2 + 1) * per)
        out[part, :] = piece[...]
        (front if k < 2 else back)[half, :] = piece[...]


LAST = (((1,), (1,)), ((), ()))
FIRST = (((0,), (0,)), ((), ()))


def stack(pieces, joined):
    at = 0
    for piece in pieces:
        joined[at : at + piece.shape[0], :] = piece[...]
        at += piece.shape[0]


def early_kernel(per, normed, cot, *refs):
    pieces, (full_t, grad, joined) = refs[:8], refs[8:]
    rows = grad.shape[0]
    g = lax.axis_index("grp")
    c = lax.axis_index("node")
    stack(pieces, joined)
    values_t = lax.dot_general(joined[...], normed[:rows, :], LAST, preferred_element_type=F32)
    for j in range(2):
        for n, block in enumerate(EARLY):
            at = (j * len(EARLY) + n) * per
            full_t[row_block(g, c, j, block, per), :] = values_t[at : at + per, :]
        for block in MID + LATE:
            full_t[row_block(g, c, j, block, per), :] = jnp.zeros((per, rows), F32)
    grad[...] = lax.dot_general(cot[...], joined[...], FIRST, preferred_element_type=F32)


def mid_kernel(per, normed, cot, w0, w1, full_t1, grad1, full_t, grad, joined):
    rows = grad.shape[0]
    g = lax.axis_index("grp")
    c = lax.axis_index("node")
    stack((w0, w1), joined)
    values_t = lax.dot_general(joined[...], normed[:rows, :], LAST, preferred_element_type=F32)
    full_t[...] = full_t1[...]
    for j in range(2):
        for n, block in enumerate(MID):
            at = (j * len(MID) + n) * per
            full_t[row_block(g, c, j, block, per), :] = values_t[at : at + per, :]
    grad[...] = grad1[...] + lax.dot_general(
        cot[...], joined[...], FIRST, preferred_element_type=F32
    )


def late_kernel(per, normed, cot, w0, w1, full_t1, grad, *refs):
    (own, g1, g2, g3), (values_far, grad_far, total_far) = refs[:4], refs[4:7]
    joined, full_t, total, values, out, sem = refs[7:]
    rows = grad.shape[0]
    half = out.shape[1] // 2
    g = lax.axis_index("grp")
    c = lax.axis_index("node")
    stores = [
        pltpu.make_async_copy(
            out.at[:, pl.ds(i * half, half)], grad_far.at[:, pl.ds(i * half, half)], sem.at[i]
        )
        for i in range(2)
    ] + [
        pltpu.make_async_copy(values, values_far, sem.at[2]),
        pltpu.make_async_copy(total, total_far, sem.at[3]),
    ]
    total[...] = own[...] + g1[...].astype(F32) + g2[...].astype(F32) + g3[...].astype(F32)
    stores[3].start()
    stack((w0, w1), joined)
    for i in range(2):
        part = slice(i * half, (i + 1) * half)
        out[:, part] = (
            grad[:, part]
            + lax.dot_general(cot[...], joined[:, part], FIRST, preferred_element_type=F32)
        ).astype(BF16)
        stores[i].start()
    values_t = lax.dot_general(joined[...], normed[:rows, :], LAST, preferred_element_type=F32)
    full_t[...] = full_t1[...]
    for j in range(2):
        for n, block in enumerate(LATE):
            at = (j * len(LATE) + n) * per
            full_t[row_block(g, c, j, block, per), :] = values_t[at : at + per, :]
    values[...] = full_t[...].T.astype(BF16)
    stores[2].start()
    for store in stores:
        store.wait()


def plain(rows, columns, dtype):
    return jax.ShapeDtypeStruct((rows, columns), dtype)


def held(rows, columns, dtype):
    return pltpu.VMEM((rows, columns), dtype)


def move(array, pairs):
    return lax.ppermute(array, AXES, pairs)


def call(kernel, outs, *args, scratch=(), far=(), far_outs=False):
    args = [
        pltpu.with_memory_space_constraint(a, pltpu.HBM if i in far else pltpu.VMEM)
        for i, a in enumerate(args)
    ]
    return pl.pallas_call(
        kernel,
        out_shape=outs,
        in_specs=[FAR if i in far else VMEM for i in range(len(args))],
        out_specs=jax.tree.map(lambda _: FAR if far_outs else VMEM, outs),
        scratch_shapes=scratch,
        compiler_params=pltpu.CompilerParams(vmem_limit_bytes=GRANT),
    )(*args)


def block_body(tokens, codes, scales, cotangent):
    return block_steps(tokens, codes, scales, cotangent)


def block_steps(tokens, codes, scales, cotangent):
    rows, width = tokens.shape
    height = cotangent.shape[1]
    per = codes.shape[0]
    quarter = 4 * per
    factor = (rows * 32) ** (-0.5)

    tokens2 = move(tokens, swap_core())
    cotangent2 = move(cotangent, swap_core())
    own, normed1, *cots = call(
        lambda *refs: own_kernel(per, *refs),
        [
            held(per, width, BF16),
            held(rows, width, BF16),
            held(24 * per, rows, F32),
            held(4 * per, rows, F32),
            held(4 * per, rows, F32),
        ],
        tokens,
        cotangent,
        codes,
        scales.T,
        scratch=[
            pltpu.VMEM((height, rows), F32),
            pltpu.VMEM((rows, width), BF16),
            pltpu.VMEM((rows, height), BF16),
            pltpu.VMEM((per, width), BF16),
            pltpu.VMEM((scales.shape[1], per), F32),
            pltpu.SemaphoreType.DMA((4,)),
        ],
        far=(0, 1, 2, 3),
    )
    sent_a, going, kept_cot, normed = call(
        lambda *refs: term_kernel(per, factor, *refs),
        [
            held(quarter, width, BF16),
            held(quarter, 2 * rows, BF16),
            held(2 * quarter, 2 * rows, BF16),
            held(2 * rows, width, BF16),
        ],
        tokens2,
        cotangent2,
        normed1,
        *cots,
        scratch=[pltpu.VMEM((height, rows), F32)],
    )
    got_a = move(sent_a, swap_first())
    by_z = [own] + [move(own, swap_z(k)) for k in (1, 2, 3)]
    sent_b, near, far, early, mid, late = call(
        lambda *refs: kept_kernel(factor, *refs),
        [
            held(quarter, width, BF16),
            held(quarter, width, F32),
            held(quarter, width, F32),
            held(24 * per, rows, BF16),
            held(4 * per, rows, BF16),
            held(4 * per, rows, BF16),
        ],
        going,
        kept_cot,
        normed,
        *cots,
    )
    got_b = move(sent_b, swap_first())
    w00, front, back = call(
        join_kernel, [held(quarter, width, BF16)] + [held(2 * per, width, BF16)] * 2, *by_z
    )
    sent2 = call(second_kernel, held(quarter, width, BF16), far, got_a)
    got2 = move(sent2, swap_second())
    w01a = move(front, swap_second())
    w01b = move(back, swap_second())
    w10 = move(w00, swap_first())
    w11a = move(w01a, swap_first())
    w11b = move(w01b, swap_first())
    v00 = move(w00, swap_core())
    v01a = move(w01a, swap_core())
    v01b = move(w01b, swap_core())
    v10 = move(w10, swap_core())

    mine, s1, s2, s3 = call(
        spread_kernel, [held(per, width, F32)] + [held(per, width, BF16)] * 3, near, got_b, got2
    )
    others = [move(s, swap_z(k)) for k, s in ((1, s1), (2, s2), (3, s3))]
    full_t, grad = call(
        lambda *refs: early_kernel(per, *refs),
        [held(height, rows, F32), held(rows, width, F32)],
        normed,
        early,
        w00,
        w01a,
        w01b,
        w10,
        v00,
        v01a,
        v01b,
        v10,
        scratch=[pltpu.VMEM((24 * per, width), BF16)],
    )
    v11a = move(w11a, swap_core())
    full_t, grad = call(
        lambda *refs: mid_kernel(per, *refs),
        [held(height, rows, F32), held(rows, width, F32)],
        normed,
        mid,
        w11a,
        v11a,
        full_t,
        grad,
        scratch=[pltpu.VMEM((4 * per, width), BF16)],
    )
    v11b = move(w11b, swap_core())
    values, input_grad, weight_grad = call(
        lambda *refs: late_kernel(per, *refs),
        [plain(rows, height, BF16), plain(rows, width, BF16), plain(per, width, F32)],
        normed,
        late,
        w11b,
        v11b,
        full_t,
        grad,
        mine,
        *others,
        scratch=[
            pltpu.VMEM((4 * per, width), BF16),
            pltpu.VMEM((height, rows), F32),
            pltpu.VMEM((per, width), F32),
            pltpu.VMEM((rows, height), BF16),
            pltpu.VMEM((rows, width), BF16),
            pltpu.SemaphoreType.DMA((4,)),
        ],
        far_outs=True,
    )
    return (values, input_grad, weight_grad)


def solution(mesh):
    sizes = dict(mesh.shape)
    blocked = (sizes["grp"], sizes["node"]) == (16, 2)
    split = P(AXES, None)
    return jax.shard_map(
        block_body if blocked else plain_body,
        mesh=mesh,
        in_specs=(split,) * 4,
        out_specs=(split,) * 3,
        check_vma=False,
    )
```

```python
import jax
import jax.numpy as jnp
from jax import lax
from jax.experimental import pallas as pl
from jax.experimental.pallas import tpu as pltpu
from jax.sharding import PartitionSpec as P


AXES = ("grp", "node")
F32 = jnp.float32
BF16 = jnp.bfloat16
VMEM = pl.BlockSpec(memory_space=pltpu.VMEM)
FAR = pl.BlockSpec(memory_space=pltpu.HBM)
GRANT = 12 * 1024 * 1024


def dequantize(block_codes, block_scales):
    count, width = block_codes.shape
    blocks = block_scales.shape[1]
    floats = (
        block_codes.astype(F32).reshape(count, blocks, -1)
        * block_scales[:, :, None]
        * width ** (-0.5)
    )
    return floats.reshape(count, -1).astype(BF16)


def plain_body(tokens, codes, scales, cotangent):
    rows_here = tokens.shape[0]
    groups = lax.axis_size("grp")
    nodes = lax.axis_size("node")
    per_device = codes.shape[0]
    height = cotangent.shape[1]
    floats = tokens.astype(F32)
    power = jnp.mean(floats * floats, axis=-1, keepdims=True)
    normed = (floats * lax.rsqrt(power + 1e-05)).astype(BF16)
    weight = lax.all_gather(dequantize(codes, scales), AXES, axis=0, tiled=True)
    values = jnp.dot(normed, weight.T, preferred_element_type=F32).astype(BF16)
    input_grad = jnp.dot(cotangent, weight, preferred_element_type=F32).astype(BF16)
    reordered = (
        cotangent.reshape(rows_here, groups, nodes, per_device)
        .transpose(0, 2, 1, 3)
        .reshape(rows_here, height)
    )
    factor = (rows_here * groups * nodes) ** (-0.5)
    term = jnp.einsum("tr,td->rd", reordered, normed, preferred_element_type=F32) * factor
    node_sum = lax.psum_scatter(
        term.astype(BF16), "node", scatter_dimension=0, tiled=True
    ).astype(F32)
    weight_grad = lax.psum_scatter(node_sum, "grp", scatter_dimension=0, tiled=True)
    return (values, input_grad, weight_grad)


def swap_first():
    return [(g * 2 + c, (g ^ (1 + c)) * 2 + c) for g in range(16) for c in range(2)]


def swap_second():
    return [(g * 2 + c, (g ^ (2 - c)) * 2 + c) for g in range(16) for c in range(2)]


def swap_z(k):
    return [(g * 2 + c, (g ^ (4 * k)) * 2 + c) for g in range(16) for c in range(2)]


def swap_core():
    return [(g * 2 + c, g * 2 + 1 - c) for g in range(16) for c in range(2)]


def row_block(g, c, j, block, per):
    core = c if j == 0 else 1 - c
    start = place_of(g, core, *PAIRS[block[0]], block[1]) * per
    return pl.ds(pl.multiple_of(start, 8), per)


def place_of(g, core, first, second, k):
    return (g ^ (first * (1 + core) + second * (2 - core) + 4 * k)) * 2 + core


PAIRS = ((0, 0), (1, 0), (0, 1), (1, 1))
EARLY = tuple((i, k) for i in (0, 2, 1) for k in range(4))
MID = ((3, 0), (3, 1))
LATE = ((3, 2), (3, 3))


def normalized(tok):
    floats = tok[...].astype(F32)
    power = jnp.mean(floats * floats, axis=-1, keepdims=True)
    return (floats * lax.rsqrt(power + 1e-05)).astype(BF16)


def own_kernel(
    per,
    tok_far,
    cot_far,
    codes_far,
    scales_far,
    weight,
    normed,
    early,
    mid,
    late,
    cot_t,
    tok,
    cot,
    codes,
    scales,
    sem,
):
    pairs = ((codes_far, codes), (scales_far, scales), (cot_far, cot), (tok_far, tok))
    loads = [pltpu.make_async_copy(x, y, sem.at[i]) for i, (x, y) in enumerate(pairs)]
    for load in loads:
        load.start()
    g = lax.axis_index("grp")
    c = lax.axis_index("node")
    width = tok.shape[1]
    blocks = scales.shape[0]
    wide = width // blocks
    inv_root = width ** (-0.5)
    loads[0].wait()
    loads[1].wait()
    by_row = scales[...].T
    for j in range(blocks):
        part = slice(j * wide, (j + 1) * wide)
        weight[:, part] = (codes[:, part].astype(F32) * by_row[:, j : j + 1] * inv_root).astype(
            BF16
        )
    loads[2].wait()
    cot_t[...] = cot[...].astype(F32).T
    loads[3].wait()
    normed[...] = normalized(tok)
    for out, blocks in ((early, EARLY), (mid, MID), (late, LATE)):
        for j in range(2):
            for n, block in enumerate(blocks):
                at = (j * len(blocks) + n) * per
                out[at : at + per, :] = cot_t[row_block(g, c, j, block, per), :]


def pick_kernel(per, cot2, early, mid, late, last, going, kept_cot, cot_t):
    quarter = 4 * per
    g = lax.axis_index("grp")
    c = lax.axis_index("node")
    cot_t[...] = cot2[...].astype(F32).T

    def both(i, own):
        swapped = [cot_t[row_block(g, c, 0, (i, k), per), :] for k in range(4)]
        return jnp.concatenate([own, jnp.concatenate(swapped, axis=0)], axis=1).astype(BF16)

    last[...] = both(3, jnp.concatenate([mid[: 2 * per, :], late[: 2 * per, :]], axis=0))
    going[...] = both(1, early[2 * quarter : 3 * quarter, :])
    kept_cot[:quarter, :] = both(0, early[:quarter, :])
    kept_cot[quarter:, :] = both(2, early[quarter : 2 * quarter, :])


def term_kernel(factor, tok2, normed1, last, sent, normed):
    rows = tok2.shape[0]
    normed[:rows, :] = normed1[...]
    normed[rows:, :] = normalized(tok2)
    sent[...] = (
        jnp.dot(last[...], normed[...], preferred_element_type=F32) * factor
    ).astype(BF16)


def kept_kernel(factor, going, kept_cot, normed, *refs):
    (early1, mid1, late1), (sent, near, far, early, mid, late) = refs[:3], refs[3:]
    half = near.shape[0]
    sent[...] = (
        jnp.dot(going[...], normed[...], preferred_element_type=F32) * factor
    ).astype(BF16)
    both = jnp.dot(kept_cot[...], normed[...], preferred_element_type=F32) * factor
    near[...] = both[:half, :]
    far[...] = both[half:, :]
    early[...] = early1[...].astype(BF16)
    mid[...] = mid1[...].astype(BF16)
    late[...] = late1[...].astype(BF16)


def second_kernel(far, got_a, sent):
    sent[...] = (far[...] + got_a[...].astype(F32)).astype(BF16)


def spread_kernel(near, got_b, got2, own, s1, s2, s3):
    per = own.shape[0]
    for k, out in enumerate((own, s1, s2, s3)):
        part = slice(k * per, (k + 1) * per)
        total = near[part, :] + got_b[part, :].astype(F32) + got2[part, :].astype(F32)
        out[...] = total.astype(out.dtype)


def join_kernel(w0, w1, w2, w3, out, front, back):
    per = w0.shape[0]
    for k, piece in enumerate((w0, w1, w2, w3)):
        part = slice(k * per, (k + 1) * per)
        half = slice(k % 2 * per, (k % 2 + 1) * per)
        out[part, :] = piece[...]
        (front if k < 2 else back)[half, :] = piece[...]


LAST = (((1,), (1,)), ((), ()))
FIRST = (((0,), (0,)), ((), ()))


def stack(pieces, joined):
    at = 0
    for piece in pieces:
        joined[at : at + piece.shape[0], :] = piece[...]
        at += piece.shape[0]


def early_kernel(per, normed, cot, *refs):
    pieces, (full_t, grad, joined) = refs[:8], refs[8:]
    rows = grad.shape[0]
    g = lax.axis_index("grp")
    c = lax.axis_index("node")
    stack(pieces, joined)
    values_t = lax.dot_general(joined[...], normed[:rows, :], LAST, preferred_element_type=F32)
    for j in range(2):
        for n, block in enumerate(EARLY):
            at = (j * len(EARLY) + n) * per
            full_t[row_block(g, c, j, block, per), :] = values_t[at : at + per, :]
        for block in MID + LATE:
            full_t[row_block(g, c, j, block, per), :] = jnp.zeros((per, rows), F32)
    grad[...] = lax.dot_general(cot[...], joined[...], FIRST, preferred_element_type=F32)


def mid_kernel(per, normed, cot, w0, w1, full_t1, grad1, full_t, grad, joined):
    rows = grad.shape[0]
    g = lax.axis_index("grp")
    c = lax.axis_index("node")
    stack((w0, w1), joined)
    values_t = lax.dot_general(joined[...], normed[:rows, :], LAST, preferred_element_type=F32)
    full_t[...] = full_t1[...]
    for j in range(2):
        for n, block in enumerate(MID):
            at = (j * len(MID) + n) * per
            full_t[row_block(g, c, j, block, per), :] = values_t[at : at + per, :]
    grad[...] = grad1[...] + lax.dot_general(
        cot[...], joined[...], FIRST, preferred_element_type=F32
    )


def late_kernel(per, normed, cot, w0, w1, full_t1, grad, *refs):
    (own, g1, g2, g3), (values_far, grad_far, total_far) = refs[:4], refs[4:7]
    joined, full_t, total, values, out, sem = refs[7:]
    rows = grad.shape[0]
    half = out.shape[1] // 2
    g = lax.axis_index("grp")
    c = lax.axis_index("node")
    stores = [
        pltpu.make_async_copy(
            out.at[:, pl.ds(i * half, half)], grad_far.at[:, pl.ds(i * half, half)], sem.at[i]
        )
        for i in range(2)
    ] + [
        pltpu.make_async_copy(values, values_far, sem.at[2]),
        pltpu.make_async_copy(total, total_far, sem.at[3]),
    ]
    total[...] = own[...] + g1[...].astype(F32) + g2[...].astype(F32) + g3[...].astype(F32)
    stores[3].start()
    stack((w0, w1), joined)
    for i in range(2):
        part = slice(i * half, (i + 1) * half)
        out[:, part] = (
            grad[:, part]
            + lax.dot_general(cot[...], joined[:, part], FIRST, preferred_element_type=F32)
        ).astype(BF16)
        stores[i].start()
    values_t = lax.dot_general(joined[...], normed[:rows, :], LAST, preferred_element_type=F32)
    full_t[...] = full_t1[...]
    for j in range(2):
        for n, block in enumerate(LATE):
            at = (j * len(LATE) + n) * per
            full_t[row_block(g, c, j, block, per), :] = values_t[at : at + per, :]
    values[...] = full_t[...].T.astype(BF16)
    stores[2].start()
    for store in stores:
        store.wait()


def plain(rows, columns, dtype):
    return jax.ShapeDtypeStruct((rows, columns), dtype)


def held(rows, columns, dtype):
    return pltpu.VMEM((rows, columns), dtype)


def move(array, pairs):
    return lax.ppermute(array, AXES, pairs)


def call(kernel, outs, *args, scratch=(), far=(), far_outs=False):
    args = [
        pltpu.with_memory_space_constraint(a, pltpu.HBM if i in far else pltpu.VMEM)
        for i, a in enumerate(args)
    ]
    return pl.pallas_call(
        kernel,
        out_shape=outs,
        in_specs=[FAR if i in far else VMEM for i in range(len(args))],
        out_specs=jax.tree.map(lambda _: FAR if far_outs else VMEM, outs),
        scratch_shapes=scratch,
        compiler_params=pltpu.CompilerParams(vmem_limit_bytes=GRANT),
    )(*args)


def block_body(tokens, codes, scales, cotangent):
    return block_steps(tokens, codes, scales, cotangent)


def block_steps(tokens, codes, scales, cotangent):
    rows, width = tokens.shape
    height = cotangent.shape[1]
    per = codes.shape[0]
    quarter = 4 * per
    factor = (rows * 32) ** (-0.5)

    tokens2 = move(tokens, swap_core())
    cotangent2 = move(cotangent, swap_core())
    own, normed1, *cots = call(
        lambda *refs: own_kernel(per, *refs),
        [
            held(per, width, BF16),
            held(rows, width, BF16),
            held(24 * per, rows, F32),
            held(4 * per, rows, F32),
            held(4 * per, rows, F32),
        ],
        tokens,
        cotangent,
        codes,
        scales.T,
        scratch=[
            pltpu.VMEM((height, rows), F32),
            pltpu.VMEM((rows, width), BF16),
            pltpu.VMEM((rows, height), BF16),
            pltpu.VMEM((per, width), BF16),
            pltpu.VMEM((scales.shape[1], per), F32),
            pltpu.SemaphoreType.DMA((4,)),
        ],
        far=(0, 1, 2, 3),
    )
    last, going, kept_cot = call(
        lambda *refs: pick_kernel(per, *refs),
        [
            held(quarter, 2 * rows, BF16),
            held(quarter, 2 * rows, BF16),
            held(2 * quarter, 2 * rows, BF16),
        ],
        cotangent2,
        *cots,
        scratch=[pltpu.VMEM((height, rows), F32)],
    )
    sent_a, normed = call(
        lambda *refs: term_kernel(factor, *refs),
        [held(quarter, width, BF16), held(2 * rows, width, BF16)],
        tokens2,
        normed1,
        last,
    )
    got_a = move(sent_a, swap_first())
    by_z = [own] + [move(own, swap_z(k)) for k in (1, 2, 3)]
    sent_b, near, far, early, mid, late = call(
        lambda *refs: kept_kernel(factor, *refs),
        [
            held(quarter, width, BF16),
            held(quarter, width, F32),
            held(quarter, width, F32),
            held(24 * per, rows, BF16),
            held(4 * per, rows, BF16),
            held(4 * per, rows, BF16),
        ],
        going,
        kept_cot,
        normed,
        *cots,
    )
    got_b = move(sent_b, swap_first())
    w00, front, back = call(
        join_kernel, [held(quarter, width, BF16)] + [held(2 * per, width, BF16)] * 2, *by_z
    )
    sent2 = call(second_kernel, held(quarter, width, BF16), far, got_a)
    got2 = move(sent2, swap_second())
    w01a = move(front, swap_second())
    w01b = move(back, swap_second())
    w10 = move(w00, swap_first())
    w11a = move(w01a, swap_first())
    w11b = move(w01b, swap_first())
    v00 = move(w00, swap_core())
    v01a = move(w01a, swap_core())
    v01b = move(w01b, swap_core())
    v10 = move(w10, swap_core())

    mine, s1, s2, s3 = call(
        spread_kernel, [held(per, width, F32)] + [held(per, width, BF16)] * 3, near, got_b, got2
    )
    others = [move(s, swap_z(k)) for k, s in ((1, s1), (2, s2), (3, s3))]
    full_t, grad = call(
        lambda *refs: early_kernel(per, *refs),
        [held(height, rows, F32), held(rows, width, F32)],
        normed,
        early,
        w00,
        w01a,
        w01b,
        w10,
        v00,
        v01a,
        v01b,
        v10,
        scratch=[pltpu.VMEM((24 * per, width), BF16)],
    )
    v11a = move(w11a, swap_core())
    full_t, grad = call(
        lambda *refs: mid_kernel(per, *refs),
        [held(height, rows, F32), held(rows, width, F32)],
        normed,
        mid,
        w11a,
        v11a,
        full_t,
        grad,
        scratch=[pltpu.VMEM((4 * per, width), BF16)],
    )
    v11b = move(w11b, swap_core())
    values, input_grad, weight_grad = call(
        lambda *refs: late_kernel(per, *refs),
        [plain(rows, height, BF16), plain(rows, width, BF16), plain(per, width, F32)],
        normed,
        late,
        w11b,
        v11b,
        full_t,
        grad,
        mine,
        *others,
        scratch=[
            pltpu.VMEM((4 * per, width), BF16),
            pltpu.VMEM((height, rows), F32),
            pltpu.VMEM((per, width), F32),
            pltpu.VMEM((rows, height), BF16),
            pltpu.VMEM((rows, width), BF16),
            pltpu.SemaphoreType.DMA((4,)),
        ],
        far_outs=True,
    )
    return (values, input_grad, weight_grad)


def solution(mesh):
    sizes = dict(mesh.shape)
    blocked = (sizes["grp"], sizes["node"]) == (16, 2)
    split = P(AXES, None)
    return jax.shard_map(
        block_body if blocked else plain_body,
        mesh=mesh,
        in_specs=(split,) * 4,
        out_specs=(split,) * 3,
        check_vma=False,
    )
```

```python
import jax
import jax.numpy as jnp
from jax import lax
from jax.experimental import pallas as pl
from jax.experimental.pallas import tpu as pltpu
from jax.sharding import PartitionSpec as P


AXES = ("grp", "node")
F32 = jnp.float32
BF16 = jnp.bfloat16
VMEM = pl.BlockSpec(memory_space=pltpu.VMEM)
FAR = pl.BlockSpec(memory_space=pltpu.HBM)
GRANT = 12 * 1024 * 1024


def dequantize(block_codes, block_scales):
    count, width = block_codes.shape
    blocks = block_scales.shape[1]
    floats = (
        block_codes.astype(F32).reshape(count, blocks, -1)
        * block_scales[:, :, None]
        * width ** (-0.5)
    )
    return floats.reshape(count, -1).astype(BF16)


def plain_body(tokens, codes, scales, cotangent):
    rows_here = tokens.shape[0]
    groups = lax.axis_size("grp")
    nodes = lax.axis_size("node")
    per_device = codes.shape[0]
    height = cotangent.shape[1]
    floats = tokens.astype(F32)
    power = jnp.mean(floats * floats, axis=-1, keepdims=True)
    normed = (floats * lax.rsqrt(power + 1e-05)).astype(BF16)
    weight = lax.all_gather(dequantize(codes, scales), AXES, axis=0, tiled=True)
    values = jnp.dot(normed, weight.T, preferred_element_type=F32).astype(BF16)
    input_grad = jnp.dot(cotangent, weight, preferred_element_type=F32).astype(BF16)
    reordered = (
        cotangent.reshape(rows_here, groups, nodes, per_device)
        .transpose(0, 2, 1, 3)
        .reshape(rows_here, height)
    )
    factor = (rows_here * groups * nodes) ** (-0.5)
    term = jnp.einsum("tr,td->rd", reordered, normed, preferred_element_type=F32) * factor
    node_sum = lax.psum_scatter(
        term.astype(BF16), "node", scatter_dimension=0, tiled=True
    ).astype(F32)
    weight_grad = lax.psum_scatter(node_sum, "grp", scatter_dimension=0, tiled=True)
    return (values, input_grad, weight_grad)


def swap_first():
    return [(g * 2 + c, (g ^ (1 + c)) * 2 + c) for g in range(16) for c in range(2)]


def swap_second():
    return [(g * 2 + c, (g ^ (2 - c)) * 2 + c) for g in range(16) for c in range(2)]


def swap_z(k):
    return [(g * 2 + c, (g ^ (4 * k)) * 2 + c) for g in range(16) for c in range(2)]


def swap_core():
    return [(g * 2 + c, g * 2 + 1 - c) for g in range(16) for c in range(2)]


def row_block(g, c, j, block, per):
    core = c if j == 0 else 1 - c
    start = place_of(g, core, *PAIRS[block[0]], block[1]) * per
    return pl.ds(pl.multiple_of(start, 8), per)


def place_of(g, core, first, second, k):
    return (g ^ (first * (1 + core) + second * (2 - core) + 4 * k)) * 2 + core


PAIRS = ((0, 0), (1, 0), (0, 1), (1, 1))
EARLY = tuple((i, k) for i in (0, 2, 1) for k in range(4))
MID = ((3, 0), (3, 1))
LATE = ((3, 2), (3, 3))


def normalized(tok):
    floats = tok[...].astype(F32)
    power = jnp.mean(floats * floats, axis=-1, keepdims=True)
    return (floats * lax.rsqrt(power + 1e-05)).astype(BF16)


def own_kernel(
    per,
    tok_far,
    cot_far,
    codes_far,
    scales_far,
    weight,
    normed,
    early,
    mid,
    late,
    cot_t,
    tok,
    cot,
    codes,
    scales,
    sem,
):
    pairs = ((codes_far, codes), (scales_far, scales), (cot_far, cot), (tok_far, tok))
    loads = [pltpu.make_async_copy(x, y, sem.at[i]) for i, (x, y) in enumerate(pairs)]
    for load in loads:
        load.start()
    g = lax.axis_index("grp")
    c = lax.axis_index("node")
    width = tok.shape[1]
    blocks = scales.shape[0]
    wide = width // blocks
    inv_root = width ** (-0.5)
    loads[0].wait()
    loads[1].wait()
    by_row = scales[...].T
    for j in range(blocks):
        part = slice(j * wide, (j + 1) * wide)
        weight[:, part] = (codes[:, part].astype(F32) * by_row[:, j : j + 1] * inv_root).astype(
            BF16
        )
    loads[2].wait()
    cot_t[...] = cot[...].astype(F32).T
    loads[3].wait()
    normed[...] = normalized(tok)
    for out, blocks in ((early, EARLY), (mid, MID), (late, LATE)):
        for j in range(2):
            for n, block in enumerate(blocks):
                at = (j * len(blocks) + n) * per
                out[at : at + per, :] = cot_t[row_block(g, c, j, block, per), :]


def pick_kernel(per, cot2, early, mid, late, last, going, kept_cot, cot_t):
    quarter = 4 * per
    g = lax.axis_index("grp")
    c = lax.axis_index("node")
    cot_t[...] = cot2[...].astype(F32).T

    def both(i, own):
        swapped = [cot_t[row_block(g, c, 0, (i, k), per), :] for k in range(4)]
        return jnp.concatenate([own, jnp.concatenate(swapped, axis=0)], axis=1).astype(BF16)

    last[...] = both(3, jnp.concatenate([mid[: 2 * per, :], late[: 2 * per, :]], axis=0))
    going[...] = both(1, early[2 * quarter : 3 * quarter, :])
    kept_cot[:quarter, :] = both(0, early[:quarter, :])
    kept_cot[quarter:, :] = both(2, early[quarter : 2 * quarter, :])


def term_kernel(factor, tok2, normed1, last, sent, normed):
    rows = tok2.shape[0]
    normed[:rows, :] = normed1[...]
    normed[rows:, :] = normalized(tok2)
    sent[...] = (
        jnp.dot(last[...], normed[...], preferred_element_type=F32) * factor
    ).astype(BF16)


def kept_kernel(factor, going, kept_cot, normed, *refs):
    (early1, mid1, late1), (sent, near, far, early, mid, late) = refs[:3], refs[3:]
    half = near.shape[0]
    sent[...] = (
        jnp.dot(going[...], normed[...], preferred_element_type=F32) * factor
    ).astype(BF16)
    both = jnp.dot(kept_cot[...], normed[...], preferred_element_type=F32) * factor
    near[...] = both[:half, :]
    far[...] = both[half:, :]
    early[...] = early1[...].astype(BF16)
    mid[...] = mid1[...].astype(BF16)
    late[...] = late1[...].astype(BF16)


def second_kernel(far, got_a, sent):
    sent[...] = (far[...] + got_a[...].astype(F32)).astype(BF16)


def spread_kernel(near, got_b, got2, own, s1, s2, s3):
    per = own.shape[0]
    for k, out in enumerate((own, s1, s2, s3)):
        part = slice(k * per, (k + 1) * per)
        total = near[part, :] + got_b[part, :].astype(F32) + got2[part, :].astype(F32)
        out[...] = total.astype(out.dtype)


def join_kernel(w0, w1, w2, w3, out, front, back):
    per = w0.shape[0]
    for k, piece in enumerate((w0, w1, w2, w3)):
        part = slice(k * per, (k + 1) * per)
        half = slice(k % 2 * per, (k % 2 + 1) * per)
        out[part, :] = piece[...]
        (front if k < 2 else back)[half, :] = piece[...]


LAST = (((1,), (1,)), ((), ()))
FIRST = (((0,), (0,)), ((), ()))


def stack(pieces, joined):
    at = 0
    for piece in pieces:
        joined[at : at + piece.shape[0], :] = piece[...]
        at += piece.shape[0]


def early_kernel(per, normed, cot, *refs):
    pieces, (full_t, grad, joined) = refs[:8], refs[8:]
    rows = grad.shape[0]
    g = lax.axis_index("grp")
    c = lax.axis_index("node")
    stack(pieces, joined)
    values_t = lax.dot_general(joined[...], normed[:rows, :], LAST, preferred_element_type=F32)
    for j in range(2):
        for n, block in enumerate(EARLY):
            at = (j * len(EARLY) + n) * per
            full_t[row_block(g, c, j, block, per), :] = values_t[at : at + per, :]
        for block in MID + LATE:
            full_t[row_block(g, c, j, block, per), :] = jnp.zeros((per, rows), F32)
    grad[...] = lax.dot_general(cot[...], joined[...], FIRST, preferred_element_type=F32)


def mid_kernel(per, normed, cot, w0, w1, full_t1, grad1, full_t, grad, joined):
    rows = grad.shape[0]
    g = lax.axis_index("grp")
    c = lax.axis_index("node")
    stack((w0, w1), joined)
    values_t = lax.dot_general(joined[...], normed[:rows, :], LAST, preferred_element_type=F32)
    full_t[...] = full_t1[...]
    for j in range(2):
        for n, block in enumerate(MID):
            at = (j * len(MID) + n) * per
            full_t[row_block(g, c, j, block, per), :] = values_t[at : at + per, :]
    grad[...] = grad1[...] + lax.dot_general(
        cot[...], joined[...], FIRST, preferred_element_type=F32
    )


def more_kernel(per, normed, cot, weight, full_t1, grad1, full_t, grad):
    rows = grad.shape[0]
    count = weight.shape[0]
    g = lax.axis_index("grp")
    c = lax.axis_index("node")
    values_t = lax.dot_general(
        weight[...], normed[:rows, :], LAST, preferred_element_type=F32
    )
    full_t[...] = full_t1[...]
    for n, block in enumerate(LATE):
        full_t[row_block(g, c, 0, block, per), :] = values_t[n * per : (n + 1) * per, :]
    grad[...] = grad1[...] + lax.dot_general(
        cot[:count, :], weight[...], FIRST, preferred_element_type=F32
    )


def late_kernel(per, normed, cot, weight, full_t1, grad, *refs):
    (own, g1, g2, g3), (values_far, grad_far, total_far) = refs[:4], refs[4:7]
    full_t, total, values, out, sem = refs[7:]
    count = weight.shape[0]
    rows = grad.shape[0]
    half = out.shape[1] // 2
    g = lax.axis_index("grp")
    c = lax.axis_index("node")
    stores = [
        pltpu.make_async_copy(
            out.at[:, pl.ds(i * half, half)], grad_far.at[:, pl.ds(i * half, half)], sem.at[i]
        )
        for i in range(2)
    ] + [
        pltpu.make_async_copy(values, values_far, sem.at[2]),
        pltpu.make_async_copy(total, total_far, sem.at[3]),
    ]
    total[...] = own[...] + g1[...].astype(F32) + g2[...].astype(F32) + g3[...].astype(F32)
    stores[3].start()
    for i in range(2):
        part = slice(i * half, (i + 1) * half)
        out[:, part] = (
            grad[:, part]
            + lax.dot_general(
                cot[count:, :], weight[:, part], FIRST, preferred_element_type=F32
            )
        ).astype(BF16)
        stores[i].start()
    values_t = lax.dot_general(
        weight[...], normed[:rows, :], LAST, preferred_element_type=F32
    )
    full_t[...] = full_t1[...]
    for n, block in enumerate(LATE):
        full_t[row_block(g, c, 1, block, per), :] = values_t[n * per : (n + 1) * per, :]
    values[...] = full_t[...].T.astype(BF16)
    stores[2].start()
    for store in stores:
        store.wait()


def plain(rows, columns, dtype):
    return jax.ShapeDtypeStruct((rows, columns), dtype)


def held(rows, columns, dtype):
    return pltpu.VMEM((rows, columns), dtype)


def move(array, pairs):
    return lax.ppermute(array, AXES, pairs)


def call(kernel, outs, *args, scratch=(), far=(), far_outs=False):
    args = [
        pltpu.with_memory_space_constraint(a, pltpu.HBM if i in far else pltpu.VMEM)
        for i, a in enumerate(args)
    ]
    return pl.pallas_call(
        kernel,
        out_shape=outs,
        in_specs=[FAR if i in far else VMEM for i in range(len(args))],
        out_specs=jax.tree.map(lambda _: FAR if far_outs else VMEM, outs),
        scratch_shapes=scratch,
        compiler_params=pltpu.CompilerParams(vmem_limit_bytes=GRANT),
    )(*args)


def block_body(tokens, codes, scales, cotangent):
    return block_steps(tokens, codes, scales, cotangent)


def block_steps(tokens, codes, scales, cotangent):
    rows, width = tokens.shape
    height = cotangent.shape[1]
    per = codes.shape[0]
    quarter = 4 * per
    factor = (rows * 32) ** (-0.5)

    tokens2 = move(tokens, swap_core())
    cotangent2 = move(cotangent, swap_core())
    own, normed1, *cots = call(
        lambda *refs: own_kernel(per, *refs),
        [
            held(per, width, BF16),
            held(rows, width, BF16),
            held(24 * per, rows, F32),
            held(4 * per, rows, F32),
            held(4 * per, rows, F32),
        ],
        tokens,
        cotangent,
        codes,
        scales.T,
        scratch=[
            pltpu.VMEM((height, rows), F32),
            pltpu.VMEM((rows, width), BF16),
            pltpu.VMEM((rows, height), BF16),
            pltpu.VMEM((per, width), BF16),
            pltpu.VMEM((scales.shape[1], per), F32),
            pltpu.SemaphoreType.DMA((4,)),
        ],
        far=(0, 1, 2, 3),
    )
    last, going, kept_cot = call(
        lambda *refs: pick_kernel(per, *refs),
        [
            held(quarter, 2 * rows, BF16),
            held(quarter, 2 * rows, BF16),
            held(2 * quarter, 2 * rows, BF16),
        ],
        cotangent2,
        *cots,
        scratch=[pltpu.VMEM((height, rows), F32)],
    )
    sent_a, normed = call(
        lambda *refs: term_kernel(factor, *refs),
        [held(quarter, width, BF16), held(2 * rows, width, BF16)],
        tokens2,
        normed1,
        last,
    )
    got_a = move(sent_a, swap_first())
    by_z = [own] + [move(own, swap_z(k)) for k in (1, 2, 3)]
    sent_b, near, far, early, mid, late = call(
        lambda *refs: kept_kernel(factor, *refs),
        [
            held(quarter, width, BF16),
            held(quarter, width, F32),
            held(quarter, width, F32),
            held(24 * per, rows, BF16),
            held(4 * per, rows, BF16),
            held(4 * per, rows, BF16),
        ],
        going,
        kept_cot,
        normed,
        *cots,
    )
    got_b = move(sent_b, swap_first())
    w00, front, back = call(
        join_kernel,
        [held(quarter, width, BF16)] + [held(2 * per, width, BF16)] * 2,
        *by_z,
    )
    sent2 = call(second_kernel, held(quarter, width, BF16), far, got_a)
    got2 = move(sent2, swap_second())
    w01a = move(front, swap_second())
    w01b = move(back, swap_second())
    w10 = move(w00, swap_first())
    w11a = move(w01a, swap_first())
    w11b = move(w01b, swap_first())
    v00 = move(w00, swap_core())
    v01a = move(w01a, swap_core())
    v01b = move(w01b, swap_core())
    v10 = move(w10, swap_core())

    mine, s1, s2, s3 = call(
        spread_kernel,
        [held(per, width, F32)] + [held(per, width, BF16)] * 3,
        near,
        got_b,
        got2,
    )
    others = [move(s, swap_z(k)) for k, s in ((1, s1), (2, s2), (3, s3))]
    full_t, grad = call(
        lambda *refs: early_kernel(per, *refs),
        [held(height, rows, F32), held(rows, width, F32)],
        normed,
        early,
        w00,
        w01a,
        w01b,
        w10,
        v00,
        v01a,
        v01b,
        v10,
        scratch=[pltpu.VMEM((24 * per, width), BF16)],
    )
    v11a = move(w11a, swap_core())
    full_t, grad = call(
        lambda *refs: mid_kernel(per, *refs),
        [held(height, rows, F32), held(rows, width, F32)],
        normed,
        mid,
        w11a,
        v11a,
        full_t,
        grad,
        scratch=[pltpu.VMEM((4 * per, width), BF16)],
    )
    v11b = move(w11b, swap_core())
    full_t, grad = call(
        lambda *refs: more_kernel(per, *refs),
        [held(height, rows, F32), held(rows, width, F32)],
        normed,
        late,
        w11b,
        full_t,
        grad,
    )
    values, input_grad, weight_grad = call(
        lambda *refs: late_kernel(per, *refs),
        [plain(rows, height, BF16), plain(rows, width, BF16), plain(per, width, F32)],
        normed,
        late,
        v11b,
        full_t,
        grad,
        mine,
        *others,
        scratch=[
            pltpu.VMEM((height, rows), F32),
            pltpu.VMEM((per, width), F32),
            pltpu.VMEM((rows, height), BF16),
            pltpu.VMEM((rows, width), BF16),
            pltpu.SemaphoreType.DMA((4,)),
        ],
        far_outs=True,
    )
    return (values, input_grad, weight_grad)


def solution(mesh):
    sizes = dict(mesh.shape)
    blocked = (sizes["grp"], sizes["node"]) == (16, 2)
    split = P(AXES, None)
    return jax.shard_map(
        block_body if blocked else plain_body,
        mesh=mesh,
        in_specs=(split,) * 4,
        out_specs=(split,) * 3,
        check_vma=False,
    )
```
